32 devices in a mesh: expert: 16 (over z, y, x), dp: 2 (over core).
Axes of the slice: x: 2, y: 2, z: 4, core: 2. Of those that a mesh axis runs over, the one named last changes fastest.
Arguments:
- events: bfloat16 [4096, 512], P(('expert', 'dp')), may hold values from -6 to 6
- gate_weights: float32 [4096, 2], P(('expert', 'dp')), may hold values from 0.1 to 1
- routes: int32 [4096, 2], P(('expert', 'dp')), may hold values from 0 to 15, all different within a row; in each aligned block of 128 rows (0 to 127, 128 to 255, ...) at most 32 rows name the same one
- session_of: int32 [4096], P(('expert', 'dp')), may hold values from 0 to 3, as said below
- partner: int32 [128], P(('expert', 'dp')), may hold values from 0 to 63, as said below
- expert_in: bfloat16 [16, 512, 1024], P('expert'), may hold values from -0.25 to 0.25
- expert_out: bfloat16 [16, 1024, 512], P('expert'), may hold values from -0.1875 to 0.1875
Outputs:
- mean_loss: float32 [], replicated
- grad_events: bfloat16 [4096, 512], P(('expert', 'dp'))
- grad_expert_in: bfloat16 [16, 512, 1024], P('expert', 'dp')
- grad_expert_out: bfloat16 [16, 1024, 512], P('expert', None, 'dp')
The draws below stay inside these ranges and needn't reach their ends.
Inputs may be any that keep to these rules, and one draw needn't show every extreme that they name: `routes`: in every aligned block of 128 events (one device's events) no expert is named by more than 32 events, a bound that some block reaches; an event's two experts differ. `session_of`: within every aligned block of 128 events the numbers never fall, start at 0 and take every value up to 3. Within every in-batch set, partner pairs the sessions: partner[partner[i]] = i and partner[i] != i.
All inputs are finite; a program needn't handle non-finite values.
Results may differ from the reference program's by a relative error of at most 0.04.
Values may be sent and summed in bfloat16 or wider, within the bound.
A program may use at most 64 MiB of HBM per device.

```python
import math
import jax
import jax.numpy as jnp
import numpy as np
from jax import lax

D = 512
FF = 1024
EV_DEV = 128
EXPERTS = 16
SES_DEV = 4
CAP = 32
EVENTS = 4096
BATCH = 64
SESSIONS = 128
N_EXPERT = 16
N_DP = 2


def draw_events(key, part):
    blocks = EVENTS // EV_DEV
    columns = BATCH // SES_DEV
    copies = SESSIONS // BATCH
    pair_count = columns // 2 * copies
    noise_key, common_key, pick_key, level_key, forced_key = jax.random.split(key, 5)
    noise = jax.random.normal(noise_key, (blocks, EV_DEV, D), jnp.float32)
    strongest = 3.0
    common = jax.random.normal(common_key, (pair_count, D), jnp.float32)
    chosen = jax.random.uniform(pick_key, (pair_count,), jnp.float32) < 0.1
    strength = jnp.exp(jax.random.uniform(level_key, (pair_count,), jnp.float32, math.log(0.3), math.log(strongest)))
    forced_at = jax.random.randint(forced_key, (copies,), 0, columns // 2).astype(jnp.int32)
    pair_ids = jnp.arange(pair_count, dtype=jnp.int32)
    forced = pair_ids // copies == forced_at[pair_ids % copies]
    level = jnp.where(forced, jnp.float32(strongest), jnp.where(chosen, strength, jnp.float32(0.0)))
    block_ids = jnp.arange(blocks, dtype=jnp.int32)
    block_pair = block_ids // copies // 2 * copies + block_ids % copies
    shared = level[block_pair][:, None] * common[block_pair]
    values = jnp.clip(noise + shared[:, None, :], -6.0, 6.0)
    return values.reshape(EVENTS, D).astype(jnp.bfloat16)


def draw_session_of(key, part):
    blocks = EVENTS // EV_DEV
    block_keys = jax.random.split(key, blocks)

    def one_block(block_key):
        order = jax.random.permutation(block_key, EV_DEV - 1) + 1
        cut_points = order[:SES_DEV - 1]
        position = jnp.arange(EV_DEV, dtype=jnp.int32)
        return jnp.sum((cut_points[None, :] <= position[:, None]).astype(jnp.int32), axis=1)
    return jax.vmap(one_block)(block_keys).reshape(EVENTS).astype(jnp.int32)


def draw_partner(key, part):
    groups = SESSIONS // BATCH
    group_keys = jax.random.split(key, groups)

    def one_group(group_key):
        order = jax.random.permutation(group_key, BATCH).astype(jnp.int32)
        even_side = order[0::2]
        odd_side = order[1::2]
        return jnp.zeros((BATCH,), jnp.int32).at[even_side].set(odd_side).at[odd_side].set(even_side)
    paired = jax.vmap(one_group)(group_keys)
    columns = BATCH // SES_DEV
    return paired.reshape(groups, columns, SES_DEV).transpose(1, 0, 2).reshape(SESSIONS).astype(jnp.int32)


def levels(rng, extent, cuts, least, high):
    gain, own = 1.0, jax.random.fold_in(rng, 6)
    for dim, parts in cuts:
        heights = jnp.exp(jax.random.uniform(jax.random.fold_in(own, dim), (parts,), jnp.float32, least / len(cuts), high / len(cuts)))
        gain = gain * jnp.repeat(heights, extent[dim] // parts).reshape([-1 if axis == dim else 1 for axis in range(len(extent))])
    return gain


def assign_block(key, own, number, rows, number_of, top, bound, skew):
    sequence = jax.random.permutation(key, number_of)
    heavy_load, usual = load_shares(number_of, rows * top, bound, skew, True), load_shares(number_of, rows * top, bound, skew, False)
    places = jnp.arange(number_of)

    def named(sizes, offset_by):
        used = int((sizes > 0).sum())
        fixed = max(1, used // 4)
        moved = fixed + (places - fixed + offset_by * (used - fixed)) % max(1, number_of - fixed)
        return jnp.zeros((number_of,), jnp.int32).at[sequence[jnp.where(places < fixed, places, moved)]].set(jnp.asarray(sizes, jnp.int32))

    sizes = jnp.where(number % 4 == 0, named(heavy_load, number // 4), named(usual, number - number // 4 - 1))
    mixed = jax.random.permutation(jax.random.fold_in(own, 3), number_of)
    giver, receiver = mixed[0:number_of // 2 * 2:2], mixed[1:number_of // 2 * 2:2]
    room = jnp.minimum(sizes[giver] - 1, bound - sizes[receiver]) // 2
    room = jnp.where((giver == sequence[0]) | (receiver == sequence[0]) | (sizes[receiver] == 0), 0, jnp.maximum(room, 0))
    moved = jax.random.randint(jax.random.fold_in(own, 4), (number_of // 2,), 0, 1 << 20) % (room + 1)
    sizes = sizes.at[giver].add(-moved).at[receiver].add(moved)
    items = jnp.searchsorted(jnp.cumsum(sizes), jnp.arange(rows * top), side="right").astype(jnp.int32)
    table = items.reshape(top, rows).T
    table = table[jax.random.permutation(jax.random.fold_in(own, 1), rows)]
    offset_by = jax.random.randint(jax.random.fold_in(own, 2), (rows, 1), 0, top)
    return jnp.take_along_axis(table, (jnp.arange(top)[None, :] + offset_by) % top, axis=1)


def load_shares(count, total, most, slope, full):
    portions = [(1 << 20) // math.isqrt(rank ** slope) + 1 for rank in range(1, count + 1)]
    largest = most if full else min(most, max(-(-total // count), total * portions[0] // sum(portions)))
    least = 1 if total - largest >= count - 1 else 0
    given, rest = [largest] + [least] * (count - 1), total - largest - least * (count - 1)
    while rest > 0:
        candidates = [i for i in range(1, count) if given[i] < largest] or [i for i in range(1, count) if given[i] < most]
        mass, left = sum([portions[i] for i in candidates]), rest
        for i in candidates:
            addition = min(most - given[i], max(1, left * portions[i] // mass), rest)
            given[i] = given[i] + addition
            rest = rest - addition
    return np.array(given)


def centred(stream_key, extent, width, bound, cuts=(), kind=jnp.bfloat16):
    entries = width * jax.random.normal(stream_key, extent, jnp.float32)
    if cuts:
        entries = entries * levels(stream_key, extent, cuts, -0.22, 0.18)
    return jnp.clip(entries, -bound, bound).astype(kind)


def setup_inputs(seed: int = 0) -> dict:
    splits = jax.random.split(jax.random.key(seed), 8)
    events = draw_events(jax.random.fold_in(splits[7], 71), 0)
    gate_weights = jnp.clip(0.1 + 0.9 * jax.random.uniform(splits[1], (EVENTS, 2), jnp.float32) ** levels(splits[1], (EVENTS, 2), ((0, 32),), -0.2, 0.2), 0.1, 1.0)
    routes_keys = jax.random.split(jax.random.fold_in(splits[2], 1), EVENTS // EV_DEV)
    routes_turns = jax.random.permutation(jax.random.fold_in(splits[2], 3), EVENTS // EV_DEV)
    routes = jax.vmap(lambda own, number: assign_block(jax.random.fold_in(splits[2], 2), own, number, EV_DEV, EXPERTS, 2, CAP, 2))(routes_keys, routes_turns).reshape((EVENTS, 2))
    session_of = draw_session_of(jax.random.fold_in(splits[7], 71), 0)
    partner = draw_partner(jax.random.fold_in(splits[7], 71), 0)
    expert_in = centred(splits[5], (EXPERTS, D, FF), D ** -0.5, 0.25, ((0, 16),))
    expert_out = centred(splits[6], (EXPERTS, FF, D), FF ** -0.5, 0.1875, ((0, 16),))
    return {"events": events, "gate_weights": gate_weights, "routes": routes, "session_of": session_of, "partner": partner, "expert_in": expert_in, "expert_out": expert_out}


TAU = 0.07
NEG = -1e+30
EPS = 1e-05

def silu_slope(preact):
    sigmoid = jax.nn.sigmoid(preact)
    return sigmoid * (1.0 + preact * (1.0 - sigmoid))

def exchange_round_sum(partials):
    rounded = partials.astype(jnp.bfloat16)
    rounded = lax.optimization_barrier(rounded)
    return lax.optimization_barrier(jnp.sum(rounded.astype(jnp.float32), axis=0)).astype(jnp.bfloat16)

def by_copies(values):
    return values.reshape((N_EXPERT, N_DP) + values.shape[1:]).transpose((1, 0) + tuple(range(2, values.ndim + 1))).reshape((N_DP, -1) + values.shape[2:])

def reference(events, gate_weights, routes, session_of, partner, expert_in, expert_out):
    blocks = EVENTS // EV_DEV
    flat_routes = routes.reshape(blocks, 2 * EV_DEV)
    onehot = (flat_routes[:, :, None] == jnp.arange(EXPERTS, dtype=jnp.int32)[None, None, :]).astype(jnp.int32)
    slot_index = lax.optimization_barrier(jnp.sum((jnp.cumsum(onehot, axis=1) - onehot) * onehot, axis=2)).astype(jnp.int32)
    block_ids = jnp.broadcast_to(jnp.arange(blocks, dtype=jnp.int32)[:, None], (blocks, 2 * EV_DEV))
    pair_ids = jnp.broadcast_to(jnp.arange(2 * EV_DEV, dtype=jnp.int32)[None, :], (blocks, 2 * EV_DEV))
    table = jnp.full((blocks, EXPERTS, CAP), -1, jnp.int32).at[block_ids, flat_routes, slot_index].set(pair_ids)
    gate_flat = gate_weights.reshape(blocks, 2 * EV_DEV)
    block_col = jnp.arange(blocks, dtype=jnp.int32)[:, None]

    def expert_rows(expert):
        pairs = table[:, expert, :]
        valid = pairs >= 0
        safe_pairs = jnp.where(valid, pairs, 0)
        event_index = block_col * EV_DEV + safe_pairs // 2
        gate_here = jnp.where(valid, gate_flat[block_col, safe_pairs], jnp.float32(0.0))
        inputs = jnp.where(valid[:, :, None], events[event_index], jnp.zeros((), jnp.bfloat16)).reshape(-1, D)
        return (event_index, gate_here, inputs)

    def forward_step(carry, expert):
        event_index, gate_here, inputs = expert_rows(expert)
        preact = jnp.dot(inputs, expert_in[expert], preferred_element_type=jnp.float32)
        hidden = jax.nn.silu(preact).astype(jnp.bfloat16)
        output = jnp.dot(hidden, expert_out[expert], preferred_element_type=jnp.float32).astype(jnp.bfloat16)
        output = output.reshape(blocks, CAP, D).astype(jnp.float32)
        return (carry.at[event_index].add(gate_here[:, :, None] * output), None)
    experts_list = jnp.arange(EXPERTS, dtype=jnp.int32)
    mixed, _ = lax.scan(forward_step, events.astype(jnp.float32), experts_list)
    member = (session_of.reshape(blocks, EV_DEV)[:, None, :] == jnp.arange(SES_DEV, dtype=jnp.int32)[None, :, None]).astype(jnp.float32)
    count = lax.optimization_barrier(jnp.sum(member, axis=2))
    pooled = jnp.einsum('bst,btd->bsd', member, mixed.reshape(blocks, EV_DEV, D), precision=lax.Precision.HIGHEST) / count[:, :, None]
    emb_float = pooled.astype(jnp.bfloat16).astype(jnp.float32)
    rscale = lax.rsqrt(lax.optimization_barrier(jnp.mean(emb_float * emb_float, axis=2)) + EPS)
    unit = emb_float * rscale[:, :, None]
    zemb = unit.astype(jnp.bfloat16)
    scale = 1.0 / (math.sqrt(D) * TAU)
    group_z = by_copies(zemb.reshape(blocks, SES_DEV, D).reshape(N_EXPERT * N_DP, SES_DEV, D)).reshape(N_DP, BATCH, D)
    group_p = partner.reshape(N_EXPERT, N_DP, SES_DEV).transpose(1, 0, 2).reshape(N_DP, BATCH)

    def group_loss(zgroup, pgroup):
        logits = jnp.dot(zgroup, zgroup.T, preferred_element_type=jnp.float32) * scale
        diagonal = jnp.eye(BATCH, dtype=jnp.bool_)
        logits = jnp.where(diagonal, NEG, logits)
        highest = lax.optimization_barrier(jnp.max(logits, axis=1))
        lse = highest + jnp.log(lax.optimization_barrier(jnp.sum(jnp.exp(logits - highest[:, None]), axis=1)))
        positive = jnp.take_along_axis(logits, pgroup[:, None], axis=1)[:, 0]
        soft = jnp.exp(logits - lse[:, None]).astype(jnp.bfloat16)
        first = jnp.dot(soft, zgroup, preferred_element_type=jnp.float32)
        second = jnp.dot(soft.T, zgroup, preferred_element_type=jnp.float32)
        dunit = scale / SESSIONS * (first + second - 2.0 * zgroup[pgroup].astype(jnp.float32))
        return (jnp.sum(lse - positive), dunit)
    loss_sums, dunit_groups = jax.vmap(group_loss)(group_z, group_p)
    mean_loss = jnp.sum(loss_sums) / SESSIONS
    dunit = dunit_groups.reshape(N_DP, N_EXPERT, SES_DEV, D).transpose(1, 0, 2, 3).reshape(blocks, SES_DEV, D)
    dpooled = rscale[:, :, None] * (dunit - unit * lax.optimization_barrier(jnp.mean(dunit * unit, axis=2, keepdims=True)))
    dmixed = jnp.einsum('bst,bsd->btd', member, dpooled / count[:, :, None], precision=lax.Precision.HIGHEST).reshape(EVENTS, D)

    def backward_step(carry, expert):
        event_index, gate_here, inputs = expert_rows(expert)
        preact = jnp.dot(inputs, expert_in[expert], preferred_element_type=jnp.float32)
        hidden = jax.nn.silu(preact).astype(jnp.bfloat16)
        grad_rows = (gate_here[:, :, None] * dmixed[event_index]).astype(jnp.bfloat16).reshape(-1, D)
        dhidden = jnp.dot(grad_rows, expert_out[expert].T, preferred_element_type=jnp.float32)
        dpre = (dhidden * silu_slope(preact)).astype(jnp.bfloat16)
        drows = jnp.dot(dpre, expert_in[expert].T, preferred_element_type=jnp.float32).astype(jnp.bfloat16)
        carry = carry.at[event_index].add(drows.reshape(blocks, CAP, D).astype(jnp.float32))
        grouped_inputs = by_copies(inputs.reshape(blocks, CAP, D)).astype(jnp.float32)
        preact_gradient_grouped = by_copies(dpre.reshape(blocks, CAP, FF)).astype(jnp.float32)
        grouped_hidden = by_copies(hidden.reshape(blocks, CAP, FF)).astype(jnp.float32)
        grouped_gradient = by_copies(grad_rows.reshape(blocks, CAP, D)).astype(jnp.float32)
        input_gradient = exchange_round_sum(jnp.einsum('oub,oup->obp', grouped_inputs, preact_gradient_grouped))
        output_gradient = exchange_round_sum(jnp.einsum('plg,pla->pga', grouped_hidden, grouped_gradient))
        return (carry, (input_gradient, output_gradient))
    dfull, (grad_expert_in, grad_expert_out) = lax.scan(backward_step, dmixed, experts_list)
    return (mean_loss, dfull.astype(jnp.bfloat16), grad_expert_in, grad_expert_out)
```

```python
import functools
import math

import jax
import jax.numpy as jnp
from jax import lax
from jax.experimental import pallas as pl
from jax.experimental.pallas import tpu as pltpu
from jax.sharding import PartitionSpec as P

TAU = 0.07
NEG = -1e30
EPS = 1e-05
MESH = pl.DeviceIdType.MESH
F32 = jnp.float32
BF16 = jnp.bfloat16
SUB = 8
COUNT_LANE = 126
PARTNER_LANE = 127


def nn(left, right):
    return lax.dot_general(left, right, (((1,), (0,)), ((), ())), preferred_element_type=F32)


def nt(left, right):
    return lax.dot_general(left, right, (((1,), (1,)), ((), ())), preferred_element_type=F32)


def tn(left, right):
    return lax.dot_general(left, right, (((0,), (0,)), ((), ())), preferred_element_type=F32)


def halves(value):
    high = value.astype(BF16)
    return high, (value - high.astype(F32)).astype(BF16)


def iota(shape, dim):
    return lax.broadcasted_iota(jnp.int32, shape, dim)


def kernel(
    n, copies, cap, sessions,
    events, gates, routes, session_of, partner, w_in, w_out,
    loss_out, ge_out, gi_final, go_final,
    select, member_s, outbox, inbox, meta_out, meta_in, block, pre, hidden,
    pool_out, pool_in, emb_out, emb_in, emb_all, dm_all, dy_s, dpre_s, back_out, back_in,
    gi_out, gi_in, go_out, go_in, loss_buf,
    x_send, x_recv, m_send, m_recv, p_send, p_recv, e_send, e_recv, d_send, d_recv,
    gi_send, gi_recv, go_send, go_recv, l_send, l_recv,
):
    me = lax.axis_index("expert")
    dp = lax.axis_index("dp")
    ev, width = events.shape
    ff = w_in.shape[1]
    half_n = n // 2
    rows = half_n * cap
    ses_rows = half_n * SUB
    my_half = me // half_n
    far = 1 - my_half

    barrier = pltpu.get_barrier_semaphore()

    def greet(k, _):
        pl.semaphore_signal(
            barrier, inc=1, device_id={"expert": lax.rem(me + k, n)}, device_id_type=MESH
        )
        return 0

    lax.fori_loop(1, n, greet, 0)
    for k in range(1, copies):
        pl.semaphore_signal(
            barrier, inc=1, device_id={"dp": lax.rem(dp + k, copies)}, device_id_type=MESH
        )

    r0, r1 = routes[0:1, :], routes[1:2, :]
    g0, g1 = gates[0:1, :], gates[1:2, :]
    ids = iota((n, ev), 0)
    one0 = jnp.where(ids == r0, 1.0, 0.0).astype(F32)
    one1 = jnp.where(ids == r1, 1.0, 0.0).astype(F32)
    before = jnp.where(iota((ev, ev), 0) < iota((ev, ev), 1), 1.0, 0.0).astype(BF16)
    prefix = nn((one0 + one1).astype(BF16), before)
    p0 = r0 * cap + jnp.sum(prefix * one0, axis=0, keepdims=True).astype(jnp.int32)
    p1 = r1 * cap + jnp.sum(prefix * one1, axis=0, keepdims=True).astype(jnp.int32)
    place = iota((n * cap, ev), 0)
    at0, at1 = place == p0, place == p1
    select[...] = jnp.where(at0 | at1, 1.0, 0.0).astype(BF16)
    gate_at = jnp.where(at0, g0, jnp.where(at1, g1, 0.0))
    outbox[...] = nn(select[...], events[...]).astype(BF16)
    member = jnp.where(iota((SUB, ev), 0) == session_of[...], 1.0, 0.0).astype(F32)
    member_s[...] = member
    counts = jnp.sum(member, axis=1, keepdims=True)
    own_partner = jnp.sum(
        jnp.where(iota((SUB, sessions), 0) == iota((SUB, sessions), 1), partner[...], 0).astype(F32),
        axis=1, keepdims=True,
    )
    gate_high, gate_low = halves(gate_at)
    member_b = member.astype(BF16)
    lane = iota((SUB, 128), 1)
    wide = nt(member_b, gate_high) + nt(member_b, gate_low)
    for e in range(n):
        group, offset = divmod(e * cap, 128)
        tile = wide[:, group * 128 : (group + 1) * 128]
        if offset:
            tile = pltpu.roll(tile, 128 - offset, 1)
        tile = jnp.where(lane < cap, tile, 0.0)
        tile = jnp.where(lane == COUNT_LANE, counts, tile)
        meta_out[e] = jnp.where(lane == PARTNER_LANE, own_partner, tile)

    pl.semaphore_wait(barrier, n - 1 + copies - 1)

    def span(e):
        return pl.ds(pl.multiple_of(e * cap, cap), cap)

    def x_copy(target, source):
        return pltpu.make_async_remote_copy(
            src_ref=outbox.at[span(target)], dst_ref=inbox.at[span(source)],
            send_sem=x_send.at[target], recv_sem=x_recv.at[source],
            device_id={"expert": target}, device_id_type=MESH,
        )

    def m_copy(target, source):
        return pltpu.make_async_remote_copy(
            src_ref=meta_out.at[target], dst_ref=meta_in.at[source],
            send_sem=m_send.at[target], recv_sem=m_recv.at[source],
            device_id={"expert": target}, device_id_type=MESH,
        )

    def p_copy(target, source):
        return pltpu.make_async_remote_copy(
            src_ref=pool_out.at[target], dst_ref=pool_in.at[source],
            send_sem=p_send.at[target], recv_sem=p_recv.at[source],
            device_id={"expert": target}, device_id_type=MESH,
        )

    def e_copy(target, source):
        return pltpu.make_async_remote_copy(
            src_ref=emb_out, dst_ref=emb_in.at[source],
            send_sem=e_send.at[target], recv_sem=e_recv.at[source],
            device_id={"expert": target}, device_id_type=MESH,
        )

    def d_copy(target, source):
        return pltpu.make_async_remote_copy(
            src_ref=back_out.at[span(target)], dst_ref=back_in.at[span(source)],
            send_sem=d_send.at[target], recv_sem=d_recv.at[source],
            device_id={"expert": target}, device_id_type=MESH,
        )

    def in_far(i):
        return far * half_n + lax.rem(me + i, half_n)

    def in_near(i):
        return my_half * half_n + lax.rem(me + i, half_n)

    def each_far(act):
        def step(i, _):
            act(in_far(i))
            return 0

        lax.fori_loop(0, half_n, step, 0)

    def each_near(act):
        def step(i, _):
            act(in_near(i))
            return 0

        lax.fori_loop(1, half_n, step, 0)

    def send_x(t):
        m_copy(t, me).start()
        x_copy(t, me).start()

    each_far(send_x)
    each_near(send_x)
    inbox[span(me), :] = outbox[span(me), :]
    meta_in[me] = meta_out[me]

    event_sum = nn(member_b, events[...])

    def wait_x(s):
        m_copy(s, s).wait_recv()
        x_copy(s, s).wait_recv()

    def forward(half):
        at = pl.ds(pl.multiple_of(half * rows, rows), rows)
        preact = nn(inbox[at, :], w_in[...])
        pre[at, :] = preact
        act = (preact / (1.0 + jnp.exp(-preact))).astype(BF16)
        hidden[at, :] = act
        y = nn(act, w_out[...]).astype(BF16)
        table = meta_in[pl.ds(half * half_n, half_n)].reshape(ses_rows, 128)
        spread = jnp.where(iota((128, rows), 0) == iota((128, rows), 1) % cap, 1.0, 0.0).astype(BF16)
        high, low = halves(table)
        full = nn(high, spread) + nn(low, spread)
        full = jnp.where(iota((ses_rows, rows), 0) // SUB == iota((ses_rows, rows), 1) // cap, full, 0.0)
        block[half] = full
        high, low = halves(full)
        part = nn(high, y) + nn(low, y)
        for j in range(half_n):
            pool_out[half * half_n + j] = part[SUB * j : SUB * j + sessions]

    each_near(wait_x)
    forward(my_half)
    each_near(lambda t: p_copy(t, me).start())
    pool_in[me] = pool_out[me]
    each_far(wait_x)
    forward(far)
    each_far(lambda t: p_copy(t, me).start())

    each_near(lambda s: p_copy(s, s).wait_recv())
    each_far(lambda s: p_copy(s, s).wait_recv())
    total = event_sum[0:sessions] + jnp.sum(pool_in[...], axis=0)
    emb = (total / counts[0:sessions]).astype(BF16).astype(F32)
    emb_out[...] = emb
    each_far(lambda t: e_copy(t, me).start())
    each_near(lambda t: e_copy(t, me).start())
    emb_in[me] = emb
    each_near(lambda s: e_copy(s, s).wait_recv())
    each_far(lambda s: e_copy(s, s).wait_recv())

    blank = jnp.zeros((SUB - sessions, width), F32)
    for e in range(n):
        emb_all[SUB * e : SUB * (e + 1), :] = jnp.concatenate([emb_in[e], blank], axis=0)
    batch = n * SUB
    emb = emb_all[...]
    scale = 1.0 / (math.sqrt(width) * TAU)
    all_sessions = n * sessions * copies
    rscale = lax.rsqrt(jnp.mean(emb * emb, axis=1, keepdims=True) + EPS)
    unit = emb * rscale
    zemb = unit.astype(BF16)
    table = meta_in[...].reshape(batch, 128)
    table_lane = iota((batch, 128), 1)
    row1 = iota((batch, 1), 0)
    real1 = row1 % SUB < sessions
    number = jnp.sum(jnp.where(table_lane == COUNT_LANE, table, 0.0), axis=1, keepdims=True)
    number = jnp.where(real1, number, 1.0)
    mate = jnp.sum(jnp.where(table_lane == PARTNER_LANE, table, 0.0), axis=1, keepdims=True)
    mate = mate.astype(jnp.int32)
    mate = mate // sessions * SUB + mate % sessions
    row = iota((batch, batch), 0)
    column = iota((batch, batch), 1)
    row_real = row % SUB < sessions
    logits = nt(zemb, zemb) * scale
    logits = jnp.where((row == column) | (column % SUB >= sessions), NEG, logits)
    highest = jnp.max(logits, axis=1, keepdims=True)
    lse = highest + jnp.log(jnp.sum(jnp.exp(logits - highest), axis=1, keepdims=True))
    is_mate = (column == mate) & row_real
    positive = jnp.sum(jnp.where(is_mate, logits, 0.0), axis=1, keepdims=True)
    loss = jnp.sum(jnp.where(real1, lse - positive, 0.0), axis=0, keepdims=True)
    loss_buf[dp] = jnp.broadcast_to(loss, (SUB, 128))
    soft = jnp.where(row_real, jnp.exp(logits - lse), 0.0).astype(BF16)
    mates = jnp.where(is_mate, 1.0, 0.0).astype(BF16)
    dunit = nn(soft, zemb) + tn(soft, zemb) - 2.0 * nn(mates, zemb)
    dunit = (scale / all_sessions) * dunit
    dpooled = rscale * (dunit - unit * jnp.mean(dunit * unit, axis=1, keepdims=True))
    dm_all[...] = dpooled / number

    def backward(half):
        at = pl.ds(pl.multiple_of(half * rows, rows), rows)
        high, low = halves(dm_all[pl.ds(pl.multiple_of(half * ses_rows, ses_rows), ses_rows), :])
        full = block[half]
        hot = jnp.where(full != 0.0, 1.0, 0.0).astype(BF16)
        dmix = tn(hot, high) + tn(hot, low)
        high, low = halves(full)
        ones = jnp.ones((ses_rows, width), BF16)
        dy = (dmix * (tn(high, ones) + tn(low, ones))).astype(BF16)
        dy_s[at, :] = dy
        preact = pre[at, :]
        sig = 1.0 / (1.0 + jnp.exp(-preact))
        dpre = (nt(dy, w_out[...]) * (sig * (1.0 + preact * (1.0 - sig)))).astype(BF16)
        dpre_s[at, :] = dpre
        back_out[at, :] = nt(dpre, w_in[...]).astype(BF16)

    backward(far)
    each_far(lambda t: d_copy(t, me).start())
    backward(my_half)
    each_near(lambda t: d_copy(t, me).start())
    back_in[span(me), :] = back_out[span(me), :]

    def dp_copies(peer, source):
        device = {"dp": peer}
        return (
            pltpu.make_async_remote_copy(
                src_ref=gi_out.at[peer], dst_ref=gi_in.at[source],
                send_sem=gi_send.at[peer], recv_sem=gi_recv.at[source],
                device_id=device, device_id_type=MESH,
            ),
            pltpu.make_async_remote_copy(
                src_ref=go_out.at[peer], dst_ref=go_in.at[source],
                send_sem=go_send.at[peer], recv_sem=go_recv.at[source],
                device_id=device, device_id_type=MESH,
            ),
            pltpu.make_async_remote_copy(
                src_ref=loss_buf.at[dp], dst_ref=loss_buf.at[source],
                send_sem=l_send.at[peer], recv_sem=l_recv.at[source],
                device_id=device, device_id_type=MESH,
            ),
        )

    peers = [lax.rem(dp + k, copies) for k in range(1, copies)]
    for peer in peers:
        dp_copies(peer, dp)[2].start()
    part = width // copies
    for c in range(copies):
        gi_out[c] = tn(inbox[:, c * part : (c + 1) * part], dpre_s[...]).astype(BF16)
    for peer in peers:
        dp_copies(peer, dp)[0].start()
    for c in range(copies):
        go_out[c] = tn(hidden[...], dy_s[:, c * part : (c + 1) * part]).astype(BF16)
    for peer in peers:
        dp_copies(peer, dp)[1].start()

    own = dm_all[pl.ds(pl.multiple_of(me * SUB, SUB), SUB), :]
    high, low = halves(own)
    member_b = member_s[...].astype(BF16)
    dmixed = tn(member_b, high) + tn(member_b, low)
    acc = gi_out[dp].astype(F32)
    for peer in peers:
        dp_copies(peer, peer)[0].wait_recv()
        acc = acc + gi_in[peer].astype(F32)
    gi_final[...] = acc.astype(BF16)
    acc = go_out[dp].astype(F32)
    for peer in peers:
        dp_copies(peer, peer)[1].wait_recv()
        acc = acc + go_in[peer].astype(F32)
    go_final[...] = acc.astype(BF16)
    for peer in peers:
        dp_copies(peer, peer)[2].wait_recv()
    loss_out[...] = (jnp.sum(loss_buf[...], axis=0) / all_sessions)[0:1, 0:1]

    each_near(lambda s: d_copy(s, s).wait_recv())
    each_far(lambda s: d_copy(s, s).wait_recv())
    ge_out[...] = (dmixed + tn(select[...], back_in[...])).astype(BF16)

    def drain(t):
        m_copy(t, me).wait_send()
        x_copy(t, me).wait_send()
        p_copy(t, me).wait_send()
        e_copy(t, me).wait_send()
        d_copy(t, me).wait_send()

    each_far(drain)
    each_near(drain)
    for peer in peers:
        for copy in dp_copies(peer, dp):
            copy.wait_send()


def body(n, copies, events, gate_weights, routes, session_of, partner, expert_in, expert_out):
    ev, width = events.shape
    ff = expert_in.shape[2]
    cap = 4 * ev // n
    sessions = partner.shape[0]
    part = width // copies
    slots = n * cap
    dma = pltpu.SemaphoreType.DMA
    vmem = pl.BlockSpec(memory_space=pltpu.VMEM)
    loss, ge, gi, go = pl.pallas_call(
        functools.partial(kernel, n, copies, cap, sessions),
        out_shape=(
            jax.ShapeDtypeStruct((1, 1), F32),
            jax.ShapeDtypeStruct((ev, width), BF16),
            jax.ShapeDtypeStruct((part, ff), BF16),
            jax.ShapeDtypeStruct((ff, part), BF16),
        ),
        in_specs=[vmem] * 7,
        out_specs=(vmem,) * 4,
        scratch_shapes=[
            pltpu.VMEM((slots, ev), BF16),
            pltpu.VMEM((SUB, ev), F32),
            pltpu.VMEM((slots, width), BF16),
            pltpu.VMEM((slots, width), BF16),
            pltpu.VMEM((n, SUB, 128), F32),
            pltpu.VMEM((n, SUB, 128), F32),
            pltpu.VMEM((2, n // 2 * SUB, slots // 2), F32),
            pltpu.VMEM((slots, ff), F32),
            pltpu.VMEM((slots, ff), BF16),
            pltpu.VMEM((n, sessions, width), F32),
            pltpu.VMEM((n, sessions, width), F32),
            pltpu.VMEM((sessions, width), F32),
            pltpu.VMEM((n, sessions, width), F32),
            pltpu.VMEM((n * SUB, width), F32),
            pltpu.VMEM((n * SUB, width), F32),
            pltpu.VMEM((slots, width), BF16),
            pltpu.VMEM((slots, ff), BF16),
            pltpu.VMEM((slots, width), BF16),
            pltpu.VMEM((slots, width), BF16),
            pltpu.VMEM((copies, part, ff), BF16),
            pltpu.VMEM((copies, part, ff), BF16),
            pltpu.VMEM((copies, ff, part), BF16),
            pltpu.VMEM((copies, ff, part), BF16),
            pltpu.VMEM((copies, SUB, 128), F32),
        ]
        + [dma((n,))] * 10
        + [dma((copies,))] * 6,
        compiler_params=pltpu.CompilerParams(collective_id=0, has_side_effects=True, vmem_limit_bytes=50 << 20),
        name="session_moe",
    )(
        events, gate_weights.T, routes.T, session_of.reshape(1, ev), partner.reshape(1, sessions),
        expert_in[0], expert_out[0],
    )
    return loss.reshape(()), ge, gi[None], go[None]


def solution(mesh):
    in_specs = (
        P(("expert", "dp"), None),
        P(("expert", "dp"), None),
        P(("expert", "dp"), None),
        P(("expert", "dp")),
        P(("expert", "dp")),
        P("expert", None, None),
        P("expert", None, None),
    )
    out_specs = (P(), P(("expert", "dp"), None), P("expert", "dp", None), P("expert", None, "dp"))
    step = functools.partial(body, mesh.shape["expert"], mesh.shape["dp"])
    return jax.shard_map(step, mesh=mesh, in_specs=in_specs, out_specs=out_specs, check_vma=False)
```

```python
import functools
import math

import jax
import jax.numpy as jnp
from jax import lax
from jax.experimental import pallas as pl
from jax.experimental.pallas import tpu as pltpu
from jax.sharding import PartitionSpec as P

TAU = 0.07
NEG = -1e30
EPS = 1e-05
MESH = pl.DeviceIdType.MESH
F32 = jnp.float32
BF16 = jnp.bfloat16
SUB = 8
VMEM_ALL = 67043328
COUNT_LANE = 126
PARTNER_LANE = 127


def nn(left, right):
    return lax.dot_general(left, right, (((1,), (0,)), ((), ())), preferred_element_type=F32)


def nt(left, right):
    return lax.dot_general(left, right, (((1,), (1,)), ((), ())), preferred_element_type=F32)


def tn(left, right):
    return lax.dot_general(left, right, (((0,), (0,)), ((), ())), preferred_element_type=F32)


def halves(value):
    high = value.astype(BF16)
    return high, (value - high.astype(F32)).astype(BF16)


def iota(shape, dim):
    return lax.broadcasted_iota(jnp.int32, shape, dim)


def kernel(
    n, copies, cap, sessions,
    events_h, gates_h, routes_h, session_h, partner_h, w_in_h, w_out_h,
    loss_out, ge_h, gi_h, go_h,
    select, member_s, outbox, inbox, meta_out, meta_in, block, pre, hidden,
    pool_out, pool_in, emb_out, emb_in, emb_all, dm_all, dy_s, dpre_s, back_out, back_in,
    gi_out, gi_in, go_out, go_in, loss_buf, gate_cols,
    events, gates, routes, session_of, partner, w_in, w_out, ge_out, gi_final, go_final, fetch, store,
    x_send, x_recv, m_send, m_recv, p_send, p_recv, e_send, e_recv, d_send, d_recv,
    gi_send, gi_recv, go_send, go_recv, l_send, l_recv,
):
    me = lax.axis_index("expert")
    dp = lax.axis_index("dp")
    ev, width = events.shape
    ff = w_in.shape[1]
    half_n = n // 2
    rows = half_n * cap
    ses_rows = half_n * SUB
    my_half = me // half_n
    far = 1 - my_half

    fetches = [
        pltpu.make_async_copy(source, target, fetch.at[i])
        for i, (source, target) in enumerate(
            (
                (routes_h, routes), (gates_h, gates), (session_h, session_of), (partner_h, partner),
                (events_h, events), (w_in_h, w_in), (w_out_h, w_out),
            )
        )
    ]
    for copy in fetches[:5]:
        copy.start()
    barrier = pltpu.get_barrier_semaphore()

    def greet(k, _):
        pl.semaphore_signal(
            barrier, inc=1, device_id={"expert": lax.rem(me + k, n)}, device_id_type=MESH
        )
        return 0

    lax.fori_loop(1, n, greet, 0)
    for k in range(1, copies):
        pl.semaphore_signal(
            barrier, inc=1, device_id={"dp": lax.rem(dp + k, copies)}, device_id_type=MESH
        )

    for copy in fetches[5:]:
        copy.start()
    for copy in fetches[:4]:
        copy.wait()

    r0, r1 = routes[0:1, :], routes[1:2, :]
    g0, g1 = gates[0:1, :], gates[1:2, :]
    ids = iota((n, ev), 0)
    one0 = jnp.where(ids == r0, 1.0, 0.0).astype(F32)
    one1 = jnp.where(ids == r1, 1.0, 0.0).astype(F32)
    before = jnp.where(iota((ev, ev), 0) < iota((ev, ev), 1), 1.0, 0.0).astype(BF16)
    prefix = nn((one0 + one1).astype(BF16), before)
    p0 = r0 * cap + jnp.sum(prefix * one0, axis=0, keepdims=True).astype(jnp.int32)
    p1 = r1 * cap + jnp.sum(prefix * one1, axis=0, keepdims=True).astype(jnp.int32)
    place = iota((n * cap, ev), 0)
    at0, at1 = place == p0, place == p1
    select[...] = jnp.where(at0 | at1, 1.0, 0.0).astype(BF16)
    gate_at = jnp.where(at0, g0, jnp.where(at1, g1, 0.0))
    fetches[4].wait()
    outbox[...] = nn(select[...], events[...]).astype(BF16)
    member = jnp.where(iota((SUB, ev), 0) == session_of[...], 1.0, 0.0).astype(F32)
    member_s[...] = member
    counts = jnp.sum(member, axis=1, keepdims=True)
    own_partner = jnp.sum(
        jnp.where(iota((SUB, sessions), 0) == iota((SUB, sessions), 1), partner[...], 0).astype(F32),
        axis=1, keepdims=True,
    )
    gate_high, gate_low = halves(gate_at)
    member_b = member.astype(BF16)
    lane = iota((SUB, 128), 1)
    wide = nt(member_b, gate_high) + nt(member_b, gate_low)
    for e in range(n):
        group, offset = divmod(e * cap, 128)
        tile = wide[:, group * 128 : (group + 1) * 128]
        if offset:
            tile = pltpu.roll(tile, 128 - offset, 1)
        tile = jnp.where(lane < cap, tile, 0.0)
        tile = jnp.where(lane == COUNT_LANE, counts, tile)
        meta_out[e] = jnp.where(lane == PARTNER_LANE, own_partner, tile)

    pl.semaphore_wait(barrier, n - 1 + copies - 1)

    def span(e):
        return pl.ds(pl.multiple_of(e * cap, cap), cap)

    def x_copy(target, source):
        return pltpu.make_async_remote_copy(
            src_ref=outbox.at[span(target)], dst_ref=inbox.at[span(source)],
            send_sem=x_send.at[target], recv_sem=x_recv.at[source],
            device_id={"expert": target}, device_id_type=MESH,
        )

    def m_copy(target, source):
        return pltpu.make_async_remote_copy(
            src_ref=meta_out.at[target], dst_ref=meta_in.at[source],
            send_sem=m_send.at[target], recv_sem=m_recv.at[source],
            device_id={"expert": target}, device_id_type=MESH,
        )

    def p_copy(target, source):
        return pltpu.make_async_remote_copy(
            src_ref=pool_out.at[target], dst_ref=pool_in.at[source],
            send_sem=p_send.at[target], recv_sem=p_recv.at[source],
            device_id={"expert": target}, device_id_type=MESH,
        )

    def e_copy(target, source):
        return pltpu.make_async_remote_copy(
            src_ref=emb_out, dst_ref=emb_in.at[source],
            send_sem=e_send.at[target], recv_sem=e_recv.at[source],
            device_id={"expert": target}, device_id_type=MESH,
        )

    def d_copy(target, source):
        return pltpu.make_async_remote_copy(
            src_ref=back_out.at[span(target)], dst_ref=back_in.at[span(source)],
            send_sem=d_send.at[target], recv_sem=d_recv.at[source],
            device_id={"expert": target}, device_id_type=MESH,
        )

    def in_far(i):
        return far * half_n + lax.rem(me + i, half_n)

    def in_near(i):
        return my_half * half_n + lax.rem(me + i, half_n)

    def each_far(act):
        def step(i, _):
            act(in_far(i))
            return 0

        lax.fori_loop(0, half_n, step, 0)

    def each_near(act):
        def step(i, _):
            act(in_near(i))
            return 0

        lax.fori_loop(1, half_n, step, 0)

    def send_x(t):
        m_copy(t, me).start()
        x_copy(t, me).start()

    each_far(send_x)
    each_near(send_x)
    inbox[span(me), :] = outbox[span(me), :]
    meta_in[me] = meta_out[me]

    event_sum = nn(member_b, events[...])

    def wait_x(s):
        m_copy(s, s).wait_recv()
        x_copy(s, s).wait_recv()

    def forward(half):
        at = pl.ds(pl.multiple_of(half * rows, rows), rows)
        preact = nn(inbox[at, :], w_in[...])
        pre[at, :] = preact
        act = (preact / (1.0 + jnp.exp(-preact))).astype(BF16)
        hidden[at, :] = act
        y = nn(act, w_out[...]).astype(BF16)
        table = meta_in[pl.ds(half * half_n, half_n)].reshape(ses_rows, 128)
        spread = jnp.where(iota((128, rows), 0) == iota((128, rows), 1) % cap, 1.0, 0.0).astype(BF16)
        high, low = halves(table)
        full = nn(high, spread) + nn(low, spread)
        full = jnp.where(iota((ses_rows, rows), 0) // SUB == iota((ses_rows, rows), 1) // cap, full, 0.0)
        block[half] = full
        high, low = halves(full)
        part = nn(high, y) + nn(low, y)
        for j in range(half_n):
            pool_out[half * half_n + j] = part[SUB * j : SUB * j + sessions].astype(BF16)

    def prepare(half):
        at = pl.ds(pl.multiple_of(half * rows, rows), rows)
        preact = pre[at, :]
        sig = 1.0 / (1.0 + jnp.exp(-preact))
        pre[at, :] = sig * (1.0 + preact * (1.0 - sig))
        high, low = halves(block[half])
        ones = jnp.ones((ses_rows, width), BF16)
        gate_cols[at, :] = tn(high, ones) + tn(low, ones)

    fetches[5].wait()
    fetches[6].wait()
    each_near(wait_x)
    forward(my_half)
    each_near(lambda t: p_copy(t, me).start())
    pool_in[me] = pool_out[me]
    prepare(my_half)
    each_far(wait_x)
    forward(far)
    each_far(lambda t: p_copy(t, me).start())
    prepare(far)

    each_near(lambda s: p_copy(s, s).wait_recv())
    each_far(lambda s: p_copy(s, s).wait_recv())
    total = event_sum[0:sessions] + jnp.sum(pool_in[...].astype(F32), axis=0)
    emb = (total / counts[0:sessions]).astype(BF16)
    emb_out[...] = emb
    each_far(lambda t: e_copy(t, me).start())
    each_near(lambda t: e_copy(t, me).start())
    emb_in[me] = emb
    each_near(lambda s: e_copy(s, s).wait_recv())
    each_far(lambda s: e_copy(s, s).wait_recv())

    blank = jnp.zeros((SUB - sessions, width), F32)
    for e in range(n):
        emb_all[SUB * e : SUB * (e + 1), :] = jnp.concatenate([emb_in[e].astype(F32), blank], axis=0)
    batch = n * SUB
    emb = emb_all[...]
    scale = 1.0 / (math.sqrt(width) * TAU)
    all_sessions = n * sessions * copies
    rscale = lax.rsqrt(jnp.mean(emb * emb, axis=1, keepdims=True) + EPS)
    unit = emb * rscale
    zemb = unit.astype(BF16)
    table = meta_in[...].reshape(batch, 128)
    table_lane = iota((batch, 128), 1)
    row1 = iota((batch, 1), 0)
    real1 = row1 % SUB < sessions
    number = jnp.sum(jnp.where(table_lane == COUNT_LANE, table, 0.0), axis=1, keepdims=True)
    number = jnp.where(real1, number, 1.0)
    mate = jnp.sum(jnp.where(table_lane == PARTNER_LANE, table, 0.0), axis=1, keepdims=True)
    mate = mate.astype(jnp.int32)
    mate = mate // sessions * SUB + mate % sessions
    row = iota((batch, batch), 0)
    column = iota((batch, batch), 1)
    row_real = row % SUB < sessions
    logits = nt(zemb, zemb) * scale
    logits = jnp.where((row == column) | (column % SUB >= sessions), NEG, logits)
    highest = jnp.max(logits, axis=1, keepdims=True)
    lse = highest + jnp.log(jnp.sum(jnp.exp(logits - highest), axis=1, keepdims=True))
    is_mate = (column == mate) & row_real
    positive = jnp.sum(jnp.where(is_mate, logits, 0.0), axis=1, keepdims=True)
    loss = jnp.sum(jnp.where(real1, lse - positive, 0.0), axis=0, keepdims=True)
    loss_buf[dp] = jnp.broadcast_to(loss, (SUB, 128))
    soft = jnp.where(row_real, jnp.exp(logits - lse), 0.0).astype(BF16)
    mates = jnp.where(is_mate, 1.0, 0.0).astype(BF16)
    dunit = nn(soft, zemb) + tn(soft, zemb) - 2.0 * nn(mates, zemb)
    dunit = (scale / all_sessions) * dunit
    dpooled = rscale * (dunit - unit * jnp.mean(dunit * unit, axis=1, keepdims=True))
    dm_all[...] = dpooled / number

    def backward(half):
        at = pl.ds(pl.multiple_of(half * rows, rows), rows)
        high, low = halves(dm_all[pl.ds(pl.multiple_of(half * ses_rows, ses_rows), ses_rows), :])
        hot = jnp.where(block[half] != 0.0, 1.0, 0.0).astype(BF16)
        dy = ((tn(hot, high) + tn(hot, low)) * gate_cols[at, :]).astype(BF16)
        dy_s[at, :] = dy
        dpre = (nt(dy, w_out[...]) * pre[at, :]).astype(BF16)
        dpre_s[at, :] = dpre
        back_out[at, :] = nt(dpre, w_in[...]).astype(BF16)

    backward(far)
    each_far(lambda t: d_copy(t, me).start())
    backward(my_half)
    each_near(lambda t: d_copy(t, me).start())
    back_in[span(me), :] = back_out[span(me), :]

    def dp_copies(peer, source):
        device = {"dp": peer}
        return (
            pltpu.make_async_remote_copy(
                src_ref=gi_out.at[peer], dst_ref=gi_in.at[source],
                send_sem=gi_send.at[peer], recv_sem=gi_recv.at[source],
                device_id=device, device_id_type=MESH,
            ),
            pltpu.make_async_remote_copy(
                src_ref=go_out.at[peer], dst_ref=go_in.at[source],
                send_sem=go_send.at[peer], recv_sem=go_recv.at[source],
                device_id=device, device_id_type=MESH,
            ),
            pltpu.make_async_remote_copy(
                src_ref=loss_buf.at[dp], dst_ref=loss_buf.at[source],
                send_sem=l_send.at[peer], recv_sem=l_recv.at[source],
                device_id=device, device_id_type=MESH,
            ),
        )

    peers = [lax.rem(dp + k, copies) for k in range(1, copies)]
    for peer in peers:
        dp_copies(peer, dp)[2].start()
    part = width // copies
    for c in range(copies):
        gi_out[c] = tn(inbox[:, c * part : (c + 1) * part], dpre_s[...]).astype(BF16)
    for peer in peers:
        dp_copies(peer, dp)[0].start()
    for c in range(copies):
        go_out[c] = tn(hidden[...], dy_s[:, c * part : (c + 1) * part]).astype(BF16)
    for peer in peers:
        dp_copies(peer, dp)[1].start()

    own = dm_all[pl.ds(pl.multiple_of(me * SUB, SUB), SUB), :]
    high, low = halves(own)
    member_b = member_s[...].astype(BF16)
    dmixed = tn(member_b, high) + tn(member_b, low)
    acc = gi_out[dp].astype(F32)
    for peer in peers:
        dp_copies(peer, peer)[0].wait_recv()
        acc = acc + gi_in[peer].astype(F32)
    gi_final[...] = acc.astype(BF16)
    stores = [
        pltpu.make_async_copy(source, target, store.at[i])
        for i, (source, target) in enumerate(((gi_final, gi_h), (go_final, go_h), (ge_out, ge_h)))
    ]
    stores[0].start()
    acc = go_out[dp].astype(F32)
    for peer in peers:
        dp_copies(peer, peer)[1].wait_recv()
        acc = acc + go_in[peer].astype(F32)
    go_final[...] = acc.astype(BF16)
    stores[1].start()
    for peer in peers:
        dp_copies(peer, peer)[2].wait_recv()
    loss_out[...] = (jnp.sum(loss_buf[...], axis=0) / all_sessions)[0:1, 0:1]

    each_near(lambda s: d_copy(s, s).wait_recv())
    each_far(lambda s: d_copy(s, s).wait_recv())
    ge_out[...] = (dmixed + tn(select[...], back_in[...])).astype(BF16)
    stores[2].start()

    def drain(t):
        m_copy(t, me).wait_send()
        x_copy(t, me).wait_send()
        p_copy(t, me).wait_send()
        e_copy(t, me).wait_send()
        d_copy(t, me).wait_send()

    each_far(drain)
    each_near(drain)
    for peer in peers:
        for copy in dp_copies(peer, dp):
            copy.wait_send()
    for copy in stores:
        copy.wait()


def export(a, b, c, a_out, b_out, c_out, a_held, b_held, c_held, sems):
    loads = [
        pltpu.make_async_copy(source, held, sems.at[i])
        for i, (source, held) in enumerate(((b, b_held), (c, c_held), (a, a_held)))
    ]
    stores = [
        pltpu.make_async_copy(held, target, sems.at[3 + i])
        for i, (held, target) in enumerate(((b_held, b_out), (c_held, c_out), (a_held, a_out)))
    ]
    for copy in loads:
        copy.start()
    for load, store in zip(loads, stores):
        load.wait()
        store.start()
    for copy in stores:
        copy.wait()


def body(n, copies, events, gate_weights, routes, session_of, partner, expert_in, expert_out):
    ev, width = events.shape
    ff = expert_in.shape[2]
    cap = 4 * ev // n
    sessions = partner.shape[0]
    part = width // copies
    slots = n * cap
    dma = pltpu.SemaphoreType.DMA
    vmem = pl.BlockSpec(memory_space=pltpu.VMEM)
    hbm = pl.BlockSpec(memory_space=pltpu.HBM)
    loss, ge, gi, go = pl.pallas_call(
        functools.partial(kernel, n, copies, cap, sessions),
        out_shape=(
            jax.ShapeDtypeStruct((1, 1), F32),
            jax.ShapeDtypeStruct((ev, width), BF16),
            jax.ShapeDtypeStruct((part, ff), BF16),
            jax.ShapeDtypeStruct((ff, part), BF16),
        ),
        in_specs=[hbm] * 7,
        out_specs=(vmem,) + (hbm,) * 3,
        scratch_shapes=[
            pltpu.VMEM((slots, ev), BF16),
            pltpu.VMEM((SUB, ev), F32),
            pltpu.VMEM((slots, width), BF16),
            pltpu.VMEM((slots, width), BF16),
            pltpu.VMEM((n, SUB, 128), F32),
            pltpu.VMEM((n, SUB, 128), F32),
            pltpu.VMEM((2, n // 2 * SUB, slots // 2), F32),
            pltpu.VMEM((slots, ff), F32),
            pltpu.VMEM((slots, ff), BF16),
            pltpu.VMEM((n, sessions, width), BF16),
            pltpu.VMEM((n, sessions, width), BF16),
            pltpu.VMEM((sessions, width), BF16),
            pltpu.VMEM((n, sessions, width), BF16),
            pltpu.VMEM((n * SUB, width), F32),
            pltpu.VMEM((n * SUB, width), F32),
            pltpu.VMEM((slots, width), BF16),
            pltpu.VMEM((slots, ff), BF16),
            pltpu.VMEM((slots, width), BF16),
            pltpu.VMEM((slots, width), BF16),
            pltpu.VMEM((copies, part, ff), BF16),
            pltpu.VMEM((copies, part, ff), BF16),
            pltpu.VMEM((copies, ff, part), BF16),
            pltpu.VMEM((copies, ff, part), BF16),
            pltpu.VMEM((copies, SUB, 128), F32),
            pltpu.VMEM((slots, width), F32),
            pltpu.VMEM((ev, width), BF16),
            pltpu.VMEM((2, ev), F32),
            pltpu.VMEM((2, ev), jnp.int32),
            pltpu.VMEM((1, ev), jnp.int32),
            pltpu.VMEM((1, sessions), jnp.int32),
            pltpu.VMEM((width, ff), BF16),
            pltpu.VMEM((ff, width), BF16),
            pltpu.VMEM((ev, width), BF16),
            pltpu.VMEM((part, ff), BF16),
            pltpu.VMEM((ff, part), BF16),
            dma((7,)),
            dma((3,)),
        ]
        + [dma((n,))] * 10
        + [dma((copies,))] * 6,
        compiler_params=pltpu.CompilerParams(collective_id=0, has_side_effects=True, vmem_limit_bytes=VMEM_ALL),
        name="session_moe",
    )(
        events, gate_weights.T, routes.T, session_of.reshape(1, ev), partner.reshape(1, sessions),
        expert_in[0], expert_out[0],
    )
    ge, gi, go = pl.pallas_call(
        export,
        out_shape=(
            jax.ShapeDtypeStruct((ev, width), BF16),
            jax.ShapeDtypeStruct((part, ff), BF16),
            jax.ShapeDtypeStruct((ff, part), BF16),
        ),
        in_specs=[hbm] * 3,
        out_specs=(hbm,) * 3,
        scratch_shapes=[
            pltpu.VMEM((ev, width), BF16), pltpu.VMEM((part, ff), BF16), pltpu.VMEM((ff, part), BF16), dma((6,)),
        ],
        compiler_params=pltpu.CompilerParams(vmem_limit_bytes=VMEM_ALL),
        name="export",
    )(ge, gi, go)
    return loss.reshape(()), ge, gi[None], go[None]


def solution(mesh):
    in_specs = (
        P(("expert", "dp"), None),
        P(("expert", "dp"), None),
        P(("expert", "dp"), None),
        P(("expert", "dp")),
        P(("expert", "dp")),
        P("expert", None, None),
        P("expert", None, None),
    )
    out_specs = (P(), P(("expert", "dp"), None), P("expert", "dp", None), P("expert", None, "dp"))
    step = functools.partial(body, mesh.shape["expert"], mesh.shape["dp"])
    return jax.shard_map(step, mesh=mesh, in_specs=in_specs, out_specs=out_specs, check_vma=False)
```

```python
import functools
import math

import jax
import jax.numpy as jnp
from jax import lax
from jax.experimental import pallas as pl
from jax.experimental.pallas import tpu as pltpu
from jax.sharding import PartitionSpec as P

TAU = 0.07
NEG = -1e30
EPS = 1e-05
MESH = pl.DeviceIdType.MESH
F32 = jnp.float32
BF16 = jnp.bfloat16
SUB = 8
VMEM_ALL = 67043328
COUNT_LANE = 126
PARTNER_LANE = 127


def nn(left, right):
    return lax.dot_general(left, right, (((1,), (0,)), ((), ())), preferred_element_type=F32)


def nt(left, right):
    return lax.dot_general(left, right, (((1,), (1,)), ((), ())), preferred_element_type=F32)


def tn(left, right):
    return lax.dot_general(left, right, (((0,), (0,)), ((), ())), preferred_element_type=F32)


def halves(value):
    high = value.astype(BF16)
    return high, (value - high.astype(F32)).astype(BF16)


def iota(shape, dim):
    return lax.broadcasted_iota(jnp.int32, shape, dim)


def kernel(
    n, copies, cap, sessions,
    events_h, gates_h, routes_h, session_h, partner_h, w_in_h, w_out_h,
    loss_out, ge_h, gi_h, go_h,
    select, member_s, outbox, inbox, meta_out, meta_in, meta_all, block, pre, hidden,
    pool_out, pool_in, emb_out, emb_in, emb_all, dm_all, dy_s, dpre_s, back_out, back_in,
    gi_out, gi_in, go_out, go_in, loss_buf, gate_cols,
    events, gates, routes, session_of, partner, w_in, w_out, ge_out, gi_final, go_final, fetch, store,
    x_send, x_recv, m_send, m_recv, p_send, p_recv, e_send, e_recv, d_send, d_recv,
    gi_send, gi_recv, go_send, go_recv, l_send, l_recv,
):
    me = lax.axis_index("expert")
    dp = lax.axis_index("dp")
    ev, width = events.shape
    ff = w_in.shape[1]
    half_n = n // 2
    rows = half_n * cap
    ses_rows = half_n * SUB
    my_half = me // half_n
    far = 1 - my_half

    fetches = [
        pltpu.make_async_copy(source, target, fetch.at[i])
        for i, (source, target) in enumerate(
            (
                (routes_h, routes), (gates_h, gates), (session_h, session_of), (partner_h, partner),
                (events_h, events), (w_in_h, w_in), (w_out_h, w_out),
            )
        )
    ]
    for copy in fetches[:5]:
        copy.start()
    barrier = pltpu.get_barrier_semaphore()

    def greet(k, _):
        pl.semaphore_signal(
            barrier, inc=1, device_id={"expert": lax.rem(me + k, n)}, device_id_type=MESH
        )
        return 0

    lax.fori_loop(1, n, greet, 0)
    for k in range(1, copies):
        pl.semaphore_signal(
            barrier, inc=1, device_id={"dp": lax.rem(dp + k, copies)}, device_id_type=MESH
        )

    for copy in fetches[5:]:
        copy.start()
    for copy in fetches[:4]:
        copy.wait()

    r0, r1 = routes[0:1, :], routes[1:2, :]
    g0, g1 = gates[0:1, :], gates[1:2, :]
    ids = iota((n, ev), 0)
    one0 = jnp.where(ids == r0, 1.0, 0.0).astype(F32)
    one1 = jnp.where(ids == r1, 1.0, 0.0).astype(F32)
    before = jnp.where(iota((ev, ev), 0) < iota((ev, ev), 1), 1.0, 0.0).astype(BF16)
    prefix = nn((one0 + one1).astype(BF16), before)
    p0 = r0 * cap + jnp.sum(prefix * one0, axis=0, keepdims=True).astype(jnp.int32)
    p1 = r1 * cap + jnp.sum(prefix * one1, axis=0, keepdims=True).astype(jnp.int32)
    place = iota((n * cap, ev), 0)
    at0, at1 = place == p0, place == p1
    select[...] = jnp.where(at0 | at1, 1.0, 0.0).astype(BF16)
    gate_at = jnp.where(at0, g0, jnp.where(at1, g1, 0.0))
    fetches[4].wait()
    outbox[...] = nn(select[...], events[...]).astype(BF16)
    member = jnp.where(iota((SUB, ev), 0) == session_of[...], 1.0, 0.0).astype(F32)
    member_s[...] = member
    member_b = member.astype(BF16)
    counts = jnp.sum(member, axis=1, keepdims=True)
    own_partner = jnp.sum(
        jnp.where(iota((SUB, sessions), 0) == iota((SUB, sessions), 1), partner[...], 0).astype(F32),
        axis=1, keepdims=True,
    )
    pl.semaphore_wait(barrier, n - 1 + copies - 1)

    def span(e):
        return pl.ds(pl.multiple_of(e * cap, cap), cap)

    def x_copy(target, source):
        return pltpu.make_async_remote_copy(
            src_ref=outbox.at[span(target)], dst_ref=inbox.at[span(source)],
            send_sem=x_send.at[target], recv_sem=x_recv.at[source],
            device_id={"expert": target}, device_id_type=MESH,
        )

    def m_copy(target, source):
        return pltpu.make_async_remote_copy(
            src_ref=meta_out.at[target], dst_ref=meta_in.at[source],
            send_sem=m_send.at[target], recv_sem=m_recv.at[source],
            device_id={"expert": target}, device_id_type=MESH,
        )

    def p_copy(target, source):
        return pltpu.make_async_remote_copy(
            src_ref=pool_out.at[target], dst_ref=pool_in.at[source],
            send_sem=p_send.at[target], recv_sem=p_recv.at[source],
            device_id={"expert": target}, device_id_type=MESH,
        )

    def e_copy(target, source):
        return pltpu.make_async_remote_copy(
            src_ref=emb_out, dst_ref=emb_in.at[source],
            send_sem=e_send.at[target], recv_sem=e_recv.at[source],
            device_id={"expert": target}, device_id_type=MESH,
        )

    def d_copy(target, source):
        return pltpu.make_async_remote_copy(
            src_ref=back_out.at[span(target)], dst_ref=back_in.at[span(source)],
            send_sem=d_send.at[target], recv_sem=d_recv.at[source],
            device_id={"expert": target}, device_id_type=MESH,
        )

    def in_far(i):
        return far * half_n + lax.rem(me + i, half_n)

    def in_near(i):
        return my_half * half_n + lax.rem(me + i, half_n)

    def each_far(act):
        def step(i, _):
            act(in_far(i))
            return 0

        lax.fori_loop(0, half_n, step, 0)

    def each_near(act):
        def step(i, _):
            act(in_near(i))
            return 0

        lax.fori_loop(1, half_n, step, 0)

    each_far(lambda t: x_copy(t, me).start())
    each_near(lambda t: x_copy(t, me).start())

    gate_high, gate_low = halves(gate_at)
    lane = iota((SUB, 128), 1)
    wide = nt(member_b, gate_high) + nt(member_b, gate_low)
    for e in range(n):
        group, offset = divmod(e * cap, 128)
        tile = wide[:, group * 128 : (group + 1) * 128]
        if offset:
            tile = pltpu.roll(tile, 128 - offset, 1)
        tile = jnp.where(lane < cap, tile, 0.0)
        tile = jnp.where(lane == COUNT_LANE, counts, tile)
        meta_out[e] = jnp.where(lane == PARTNER_LANE, own_partner, tile)[0:sessions]
    each_far(lambda t: m_copy(t, me).start())
    each_near(lambda t: m_copy(t, me).start())
    inbox[span(me), :] = outbox[span(me), :]
    meta_in[me] = meta_out[me]
    no_rows = jnp.zeros((SUB - sessions, 128), F32)

    event_sum = nn(member_b, events[...])

    def wait_x(s):
        m_copy(s, s).wait_recv()
        x_copy(s, s).wait_recv()

    def forward(half):
        at = pl.ds(pl.multiple_of(half * rows, rows), rows)
        preact = nn(inbox[at, :], w_in[...])
        pre[at, :] = preact
        act = (preact / (1.0 + jnp.exp(-preact))).astype(BF16)
        hidden[at, :] = act
        y = nn(act, w_out[...]).astype(BF16)
        for j in range(half_n):
            e = half * half_n + j
            meta_all[e] = jnp.concatenate([meta_in[e], no_rows], axis=0)
        table = meta_all[pl.ds(half * half_n, half_n)].reshape(ses_rows, 128)
        spread = jnp.where(iota((128, rows), 0) == iota((128, rows), 1) % cap, 1.0, 0.0).astype(BF16)
        high, low = halves(table)
        full = nn(high, spread) + nn(low, spread)
        full = jnp.where(iota((ses_rows, rows), 0) // SUB == iota((ses_rows, rows), 1) // cap, full, 0.0)
        block[half] = full
        high, low = halves(full)
        part = nn(high, y) + nn(low, y)
        for j in range(half_n):
            pool_out[half * half_n + j] = part[SUB * j : SUB * j + sessions].astype(BF16)

    def prepare(half):
        at = pl.ds(pl.multiple_of(half * rows, rows), rows)
        preact = pre[at, :]
        sig = 1.0 / (1.0 + jnp.exp(-preact))
        pre[at, :] = sig * (1.0 + preact * (1.0 - sig))
        high, low = halves(block[half])
        ones = jnp.ones((ses_rows, width), BF16)
        gate_cols[at, :] = tn(high, ones) + tn(low, ones)

    fetches[5].wait()
    fetches[6].wait()
    each_near(wait_x)
    forward(my_half)
    each_near(lambda t: p_copy(t, me).start())
    pool_in[me] = pool_out[me]
    prepare(my_half)
    each_far(wait_x)
    forward(far)
    each_far(lambda t: p_copy(t, me).start())
    prepare(far)

    each_near(lambda s: p_copy(s, s).wait_recv())
    each_far(lambda s: p_copy(s, s).wait_recv())
    total = event_sum[0:sessions] + jnp.sum(pool_in[...].astype(F32), axis=0)
    emb = (total / counts[0:sessions]).astype(BF16)
    emb_out[...] = emb
    each_far(lambda t: e_copy(t, me).start())
    each_near(lambda t: e_copy(t, me).start())
    emb_in[me] = emb
    each_near(lambda s: e_copy(s, s).wait_recv())
    each_far(lambda s: e_copy(s, s).wait_recv())

    blank = jnp.zeros((SUB - sessions, width), F32)
    for e in range(n):
        emb_all[SUB * e : SUB * (e + 1), :] = jnp.concatenate([emb_in[e].astype(F32), blank], axis=0)
    batch = n * SUB
    emb = emb_all[...]
    scale = 1.0 / (math.sqrt(width) * TAU)
    all_sessions = n * sessions * copies
    rscale = lax.rsqrt(jnp.mean(emb * emb, axis=1, keepdims=True) + EPS)
    unit = emb * rscale
    zemb = unit.astype(BF16)
    table = meta_all[...].reshape(batch, 128)
    table_lane = iota((batch, 128), 1)
    row1 = iota((batch, 1), 0)
    real1 = row1 % SUB < sessions
    number = jnp.sum(jnp.where(table_lane == COUNT_LANE, table, 0.0), axis=1, keepdims=True)
    number = jnp.where(real1, number, 1.0)
    mate = jnp.sum(jnp.where(table_lane == PARTNER_LANE, table, 0.0), axis=1, keepdims=True)
    mate = mate.astype(jnp.int32)
    mate = mate // sessions * SUB + mate % sessions
    row = iota((batch, batch), 0)
    column = iota((batch, batch), 1)
    row_real = row % SUB < sessions
    logits = nt(zemb, zemb) * scale
    logits = jnp.where((row == column) | (column % SUB >= sessions), NEG, logits)
    highest = jnp.max(logits, axis=1, keepdims=True)
    lse = highest + jnp.log(jnp.sum(jnp.exp(logits - highest), axis=1, keepdims=True))
    is_mate = (column == mate) & row_real
    positive = jnp.sum(jnp.where(is_mate, logits, 0.0), axis=1, keepdims=True)
    loss = jnp.sum(jnp.where(real1, lse - positive, 0.0), axis=0, keepdims=True)
    loss_buf[dp] = jnp.broadcast_to(loss, (SUB, 128))
    soft = jnp.where(row_real, jnp.exp(logits - lse), 0.0).astype(BF16)
    mates = jnp.where(is_mate, 1.0, 0.0).astype(BF16)
    dunit = nn(soft, zemb) + tn(soft, zemb) - 2.0 * nn(mates, zemb)
    dunit = (scale / all_sessions) * dunit
    dpooled = rscale * (dunit - unit * jnp.mean(dunit * unit, axis=1, keepdims=True))
    dm_all[...] = dpooled / number

    q_rows, q_ses, q_n = rows // 2, ses_rows // 2, half_n // 2

    def backward(half, q):
        at = pl.ds(pl.multiple_of(half * rows + q * q_rows, q_rows), q_rows)
        high, low = halves(dm_all[pl.ds(pl.multiple_of(half * ses_rows + q * q_ses, q_ses), q_ses), :])
        full = block[half, q * q_ses : (q + 1) * q_ses, q * q_rows : (q + 1) * q_rows]
        hot = jnp.where(full != 0.0, 1.0, 0.0).astype(BF16)
        dy = ((tn(hot, high) + tn(hot, low)) * gate_cols[at, :]).astype(BF16)
        dy_s[at, :] = dy
        dpre = (nt(dy, w_out[...]) * pre[at, :]).astype(BF16)
        dpre_s[at, :] = dpre
        back_out[at, :] = nt(dpre, w_in[...]).astype(BF16)

    def send_quarter(q):
        def step(i, _):
            d_copy(far * half_n + q * q_n + lax.rem(me + i, q_n), me).start()
            return 0

        lax.fori_loop(0, q_n, step, 0)

    for q in range(2):
        backward(far, q)
        send_quarter(q)
    for q in range(2):
        backward(my_half, q)
    each_near(lambda t: d_copy(t, me).start())
    back_in[span(me), :] = back_out[span(me), :]

    def dp_copies(peer, source):
        device = {"dp": peer}
        return (
            pltpu.make_async_remote_copy(
                src_ref=gi_out.at[peer], dst_ref=gi_in.at[source],
                send_sem=gi_send.at[peer], recv_sem=gi_recv.at[source],
                device_id=device, device_id_type=MESH,
            ),
            pltpu.make_async_remote_copy(
                src_ref=go_out.at[peer], dst_ref=go_in.at[source],
                send_sem=go_send.at[peer], recv_sem=go_recv.at[source],
                device_id=device, device_id_type=MESH,
            ),
            pltpu.make_async_remote_copy(
                src_ref=loss_buf.at[dp], dst_ref=loss_buf.at[source],
                send_sem=l_send.at[peer], recv_sem=l_recv.at[source],
                device_id=device, device_id_type=MESH,
            ),
        )

    peers = [lax.rem(dp + k, copies) for k in range(1, copies)]
    for peer in peers:
        dp_copies(peer, dp)[2].start()
    part = width // copies
    for c in range(copies):
        gi_out[c] = tn(inbox[:, c * part : (c + 1) * part], dpre_s[...]).astype(BF16)
    for peer in peers:
        dp_copies(peer, dp)[0].start()
    for c in range(copies):
        go_out[c] = tn(hidden[...], dy_s[:, c * part : (c + 1) * part]).astype(BF16)
    for peer in peers:
        dp_copies(peer, dp)[1].start()

    own = dm_all[pl.ds(pl.multiple_of(me * SUB, SUB), SUB), :]
    high, low = halves(own)
    member_b = member_s[...].astype(BF16)
    dmixed = tn(member_b, high) + tn(member_b, low)
    acc = gi_out[dp].astype(F32)
    for peer in peers:
        dp_copies(peer, peer)[0].wait_recv()
        acc = acc + gi_in[peer].astype(F32)
    gi_final[...] = acc.astype(BF16)
    stores = [
        pltpu.make_async_copy(source, target, store.at[i])
        for i, (source, target) in enumerate(((gi_final, gi_h), (go_final, go_h), (ge_out, ge_h)))
    ]
    stores[0].start()
    acc = go_out[dp].astype(F32)
    for peer in peers:
        dp_copies(peer, peer)[1].wait_recv()
        acc = acc + go_in[peer].astype(F32)
    go_final[...] = acc.astype(BF16)
    stores[1].start()
    for peer in peers:
        dp_copies(peer, peer)[2].wait_recv()
    loss_out[...] = (jnp.sum(loss_buf[...], axis=0) / all_sessions)[0:1, 0:1]

    each_near(lambda s: d_copy(s, s).wait_recv())
    each_far(lambda s: d_copy(s, s).wait_recv())
    ge_out[...] = (dmixed + tn(select[...], back_in[...])).astype(BF16)
    stores[2].start()

    def drain(t):
        m_copy(t, me).wait_send()
        x_copy(t, me).wait_send()
        p_copy(t, me).wait_send()
        e_copy(t, me).wait_send()
        d_copy(t, me).wait_send()

    each_far(drain)
    each_near(drain)
    for peer in peers:
        for copy in dp_copies(peer, dp):
            copy.wait_send()
    for copy in stores:
        copy.wait()


def export(a, b, c, a_out, b_out, c_out, a_held, b_held, c_held, sems):
    loads = [
        pltpu.make_async_copy(source, held, sems.at[i])
        for i, (source, held) in enumerate(((b, b_held), (c, c_held), (a, a_held)))
    ]
    stores = [
        pltpu.make_async_copy(held, target, sems.at[3 + i])
        for i, (held, target) in enumerate(((b_held, b_out), (c_held, c_out), (a_held, a_out)))
    ]
    for copy in loads:
        copy.start()
    for load, store in zip(loads, stores):
        load.wait()
        store.start()
    for copy in stores:
        copy.wait()


def body(n, copies, events, gate_weights, routes, session_of, partner, expert_in, expert_out):
    ev, width = events.shape
    ff = expert_in.shape[2]
    cap = 4 * ev // n
    sessions = partner.shape[0]
    part = width // copies
    slots = n * cap
    dma = pltpu.SemaphoreType.DMA
    vmem = pl.BlockSpec(memory_space=pltpu.VMEM)
    hbm = pl.BlockSpec(memory_space=pltpu.HBM)
    loss, ge, gi, go = pl.pallas_call(
        functools.partial(kernel, n, copies, cap, sessions),
        out_shape=(
            jax.ShapeDtypeStruct((1, 1), F32),
            jax.ShapeDtypeStruct((ev, width), BF16),
            jax.ShapeDtypeStruct((part, ff), BF16),
            jax.ShapeDtypeStruct((ff, part), BF16),
        ),
        in_specs=[hbm] * 7,
        out_specs=(vmem,) + (hbm,) * 3,
        scratch_shapes=[
            pltpu.VMEM((slots, ev), BF16),
            pltpu.VMEM((SUB, ev), F32),
            pltpu.VMEM((slots, width), BF16),
            pltpu.VMEM((slots, width), BF16),
            pltpu.VMEM((n, sessions, 128), F32),
            pltpu.VMEM((n, sessions, 128), F32),
            pltpu.VMEM((n, SUB, 128), F32),
            pltpu.VMEM((2, n // 2 * SUB, slots // 2), F32),
            pltpu.VMEM((slots, ff), F32),
            pltpu.VMEM((slots, ff), BF16),
            pltpu.VMEM((n, sessions, width), BF16),
            pltpu.VMEM((n, sessions, width), BF16),
            pltpu.VMEM((sessions, width), BF16),
            pltpu.VMEM((n, sessions, width), BF16),
            pltpu.VMEM((n * SUB, width), F32),
            pltpu.VMEM((n * SUB, width), F32),
            pltpu.VMEM((slots, width), BF16),
            pltpu.VMEM((slots, ff), BF16),
            pltpu.VMEM((slots, width), BF16),
            pltpu.VMEM((slots, width), BF16),
            pltpu.VMEM((copies, part, ff), BF16),
            pltpu.VMEM((copies, part, ff), BF16),
            pltpu.VMEM((copies, ff, part), BF16),
            pltpu.VMEM((copies, ff, part), BF16),
            pltpu.VMEM((copies, SUB, 128), F32),
            pltpu.VMEM((slots, width), F32),
            pltpu.VMEM((ev, width), BF16),
            pltpu.VMEM((2, ev), F32),
            pltpu.VMEM((2, ev), jnp.int32),
            pltpu.VMEM((1, ev), jnp.int32),
            pltpu.VMEM((1, sessions), jnp.int32),
            pltpu.VMEM((width, ff), BF16),
            pltpu.VMEM((ff, width), BF16),
            pltpu.VMEM((ev, width), BF16),
            pltpu.VMEM((part, ff), BF16),
            pltpu.VMEM((ff, part), BF16),
            dma((7,)),
            dma((3,)),
        ]
        + [dma((n,))] * 10
        + [dma((copies,))] * 6,
        compiler_params=pltpu.CompilerParams(collective_id=0, has_side_effects=True, vmem_limit_bytes=VMEM_ALL),
        name="session_moe",
    )(
        events, gate_weights.T, routes.T, session_of.reshape(1, ev), partner.reshape(1, sessions),
        expert_in[0], expert_out[0],
    )
    ge, gi, go = pl.pallas_call(
        export,
        out_shape=(
            jax.ShapeDtypeStruct((ev, width), BF16),
            jax.ShapeDtypeStruct((part, ff), BF16),
            jax.ShapeDtypeStruct((ff, part), BF16),
        ),
        in_specs=[hbm] * 3,
        out_specs=(hbm,) * 3,
        scratch_shapes=[
            pltpu.VMEM((ev, width), BF16), pltpu.VMEM((part, ff), BF16), pltpu.VMEM((ff, part), BF16), dma((6,)),
        ],
        compiler_params=pltpu.CompilerParams(vmem_limit_bytes=VMEM_ALL),
        name="export",
    )(ge, gi, go)
    return loss.reshape(()), ge, gi[None], go[None]


def solution(mesh):
    in_specs = (
        P(("expert", "dp"), None),
        P(("expert", "dp"), None),
        P(("expert", "dp"), None),
        P(("expert", "dp")),
        P(("expert", "dp")),
        P("expert", None, None),
        P("expert", None, None),
    )
    out_specs = (P(), P(("expert", "dp"), None), P("expert", "dp", None), P("expert", None, "dp"))
    step = functools.partial(body, mesh.shape["expert"], mesh.shape["dp"])
    return jax.shard_map(step, mesh=mesh, in_specs=in_specs, out_specs=out_specs, check_vma=False)
```
